128 devices in a mesh: run: 8 (over y_hi, z), cell: 16 (over x, y_lo, core).
Axes of the slice: x: 4, y: 4 (y_hi: 2, y_lo: 2; y = y_hi * 2 + y_lo), z: 4, core: 2. Of those that a mesh axis runs over, the one named last changes fastest.
Arguments:
- outputs: bfloat16 [4096, 4, 4096], P('run', None, 'cell'), may hold values from -6 to 6
- run_precision: bfloat16 [4096, 4096], P('run', 'cell'), as said below
- line_precision: bfloat16 [4096, 4096], P(None, 'cell'), as said below
Outputs:
- weights: bfloat16 [4096, 4, 4096], P('run', None, 'cell')
The draws below stay inside these ranges and needn't reach their ends.
Inputs may be any that keep to these rules, and one draw needn't show every extreme that they name: run_precision is symmetric. line_precision is symmetric.
All inputs are finite; a program needn't handle non-finite values.
Results may differ from the reference program's by a relative error of at most 0.0049.
Values may be sent and summed in bfloat16 or wider, within the bound.
No kernel may reach another device: no remote copies, remote signals or barrier semaphores. Data moves between devices by JAX's collectives and lax.ppermute only.
A program may use at most 128 MiB of HBM per device.

```python
import math
import jax
import jax.numpy as jnp

RUNS = 4096
NY = 4096
LINES = 4


def precision_matrix(key, order):
    first, second = jax.random.split(key, 2)
    noise = jax.random.normal(first, (order, order), jnp.float32) * math.sqrt(0.5 / order)
    symmetric = (noise + noise.T) * math.sqrt(0.5)
    diagonal = jax.random.uniform(second, (order,), jnp.float32, 0.5, 1.5)
    matrix = symmetric + jnp.diag(diagonal)
    return matrix.astype(jnp.bfloat16)


def draw_run_precision(key, part):
    return precision_matrix(jax.random.fold_in(key, 11), RUNS)


def draw_line_precision(key, part):
    return precision_matrix(jax.random.fold_in(key, 23), NY)


def block_levels(key, dims, cuts, low, high):
    loudness, own = 1.0, jax.random.fold_in(key, 6)
    for axis_at, shards_of in cuts:
        draws = jnp.exp(jax.random.uniform(jax.random.fold_in(own, axis_at), (shards_of,), jnp.float32, low / len(cuts), high / len(cuts)))
        loudness = loudness * jnp.repeat(draws, dims[axis_at] // shards_of).reshape([-1 if axis == axis_at else 1 for axis in range(len(dims))])
    return loudness


def gaussian(stream_key, shape, width, bound, cuts=(), dtype=jnp.bfloat16):
    factor_of = block_levels(stream_key, shape, cuts, -0.22, 0.18) if cuts else 1.0
    result = jax.random.normal(stream_key, shape, jnp.float32) * width * factor_of
    return jnp.minimum(jnp.maximum(result, -bound), bound).astype(dtype)


def setup_inputs(seed: int = 0) -> dict:
    seeds = jax.random.split(jax.random.key(seed), 4)
    return {
        "outputs": gaussian(seeds[0], (RUNS, LINES, NY), 1.0, 6.0, ((0, 8), (2, 16))),
        "run_precision": draw_run_precision(jax.random.fold_in(seeds[3], 71), 0),
        "line_precision": draw_line_precision(jax.random.fold_in(seeds[3], 71), 0),
    }


def reference(outputs, run_precision, line_precision):
    flat_cells = outputs.reshape(RUNS, LINES * NY)
    middle = jnp.dot(run_precision, flat_cells, preferred_element_type=jnp.float32).astype(jnp.bfloat16)
    weighted = jnp.dot(middle.reshape(RUNS * LINES, NY), line_precision, preferred_element_type=jnp.float32)
    return weighted.astype(jnp.bfloat16).reshape(RUNS, LINES, NY)
```

```python
import jax
import jax.numpy as jnp
from jax import lax
from jax.experimental import pallas as pl
from jax.experimental.pallas import tpu as pltpu
from jax.sharding import PartitionSpec as P

AXES = ("run", "cell")


def coords(i):
    run, cell = divmod(i, 16)
    return run // 4, run % 4, cell // 4, (cell // 2) % 2, cell % 2


def index(yh, z, x, yl, core):
    return (yh * 4 + z % 4) * 16 + (x % 4) * 4 + yl * 2 + core


def send(value, dz=0, dx=0, yh=0, yl=0, core=0):
    pairs = []
    for i in range(128):
        h, z, x, l, c = coords(i)
        pairs.append((i, index(h ^ yh, z + dz, x + dx, l ^ yl, c ^ core)))
    return lax.ppermute(value, AXES, pairs)


def gather(own, side):
    if side == "run":
        ring = lambda v, d: send(v, dz=d)
        across = lambda v: send(v, yh=1)
    else:
        ring = lambda v, d: send(v, dx=d)
        across = lambda v: send(v, yl=1)
    partner = across(own)
    below, above = ring(own, 1), ring(own, -1)
    far = ring(below, 1)
    p_below, p_above = ring(partner, 1), ring(partner, -1)
    p_far = ring(p_above, -1)
    return (
        [(own, 0, 0), (below, -1, 0), (above, 1, 0)],
        [(partner, 0, 1), (far, 2, 0), (p_above, 1, 1)],
        [(p_below, -1, 1), (p_far, 2, 1)],
    )


def product(pieces, blocks, matrix, total, last, left):
    n = len(pieces)
    steps, rows, width = 2, 256, 512

    def kernel(at, *refs):
        chunks, mats, rest = refs[:n], refs[n : 2 * n], refs[2 * n :]
        acc = rest[0][...] if total is not None else jnp.zeros((rows, width), jnp.float32)
        for chunk, mat in zip(chunks, mats):
            a, b = (mat, chunk) if left else (chunk, mat)
            acc = acc + jnp.dot(a[...], b[...], preferred_element_type=jnp.float32)
        rest[-1][...] = acc.astype(rest[-1].dtype)

    tile = pl.BlockSpec((rows, width), lambda i, at: (i, 0))
    full = pl.BlockSpec((width, width), lambda i, at: (0, 0))
    if left:
        chunk_specs = [full] * n
        mat_specs = [pl.BlockSpec((rows, width), lambda i, at, j=j: (i, at[j])) for j in range(n)]
    else:
        chunk_specs = [tile] * n
        mat_specs = [pl.BlockSpec((width, width), lambda i, at, j=j: (at[j], 0)) for j in range(n)]
    totals = [] if total is None else [total]
    return pl.pallas_call(
        kernel,
        out_shape=jax.ShapeDtypeStruct((512, 512), jnp.bfloat16 if last else jnp.float32),
        grid_spec=pltpu.PrefetchScalarGridSpec(
            num_scalar_prefetch=1,
            grid=(steps,),
            in_specs=chunk_specs + mat_specs + [tile] * len(totals),
            out_specs=tile,
        ),
        compiler_params=pltpu.CompilerParams(vmem_limit_bytes=32 << 20),
        cost_estimate=pl.CostEstimate(
            flops=2 * 512**3 * n, transcendentals=0, bytes_accessed=(n + 1) * (1 << 20)
        ),
        name="product_" + ("left" if left else "right"),
    )(jnp.stack(blocks).astype(jnp.int32), *pieces, *[matrix] * n, *totals)


def apply(groups, side, matrix):
    run, cell = lax.axis_index("run"), lax.axis_index("cell")
    if side == "run":
        block = lambda d, p: ((run & 4) ^ 4 * p) | (run + d & 3)
    else:
        block = lambda d, p: ((cell >> 2) + d & 3) << 1 | (cell >> 1 & 1) ^ p
    total = None
    for k, group in enumerate(groups):
        total = product(
            [c for c, _, _ in group],
            [block(d, p) for _, d, p in group],
            matrix,
            total,
            k == len(groups) - 1,
            side == "run",
        )
    return total


def per_device(outputs, run_precision, line_precision):
    core = lax.axis_index("cell") & 1
    first = core == 0
    rows = lax.all_gather(run_precision, "cell", axis=1, tiled=True)
    lines = jnp.transpose(outputs, (1, 0, 2))
    mine = lax.dynamic_slice_in_dim(lines, 2 * core, 2, 0)
    theirs = send(lax.dynamic_slice_in_dim(lines, 2 - 2 * core, 2, 0), core=1)
    chunk = jnp.concatenate([jnp.where(first, mine, theirs), jnp.where(first, theirs, mine)], axis=2)
    columns = jnp.concatenate([line_precision, send(line_precision, core=1)], axis=1)

    gathered_a = gather(chunk[0], "run")
    gathered_b = gather(chunk[1], "cell")
    mid_b = apply(gathered_b, "cell", columns)
    mid_a = apply(gathered_a, "run", rows)
    gathered_b = gather(mid_b, "run")
    gathered_a = gather(mid_a, "cell")
    out_b = apply(gathered_b, "run", rows)
    out_a = apply(gathered_a, "cell", columns)

    got_a, got_b = send(out_a[:, 256:], core=1), send(out_b[:, 256:], core=1)
    kept = jnp.stack([out_a[:, :256], out_b[:, :256]], axis=1)
    got = jnp.stack([got_a, got_b], axis=1)
    return jnp.concatenate([jnp.where(first, kept, got), jnp.where(first, got, kept)], axis=1)


def solution(mesh):
    placed = (P("run", None, "cell"), P("run", "cell"), P(None, "cell"))
    return jax.shard_map(
        per_device, mesh=mesh, in_specs=placed, out_specs=P("run", None, "cell"), check_vma=False
    )
```

```python
import jax
import jax.numpy as jnp
from jax import lax
from jax.experimental import pallas as pl
from jax.experimental.pallas import tpu as pltpu
from jax.sharding import PartitionSpec as P

AXES = ("run", "cell")


def coords(i):
    run, cell = divmod(i, 16)
    return run // 4, run % 4, cell // 4, (cell // 2) % 2, cell % 2


def index(yh, z, x, yl, core):
    return (yh * 4 + z % 4) * 16 + (x % 4) * 4 + yl * 2 + core


def hbm(value):
    return pltpu.with_memory_space_constraint(value, pltpu.HBM)


def send(value, dx=0, yl=0, core=0):
    pairs = []
    for i in range(128):
        h, z, x, l, c = coords(i)
        pairs.append((i, index(h, z, x + dx, l ^ yl, c ^ core)))
    return lax.ppermute(value, AXES, pairs)


def sign(stream):
    return 1 - 2 * (stream // 2)


def ring(value, stream, step):
    step = step * sign(stream)
    pairs = []
    for i in range(128):
        h, z, x, l, c = coords(i)
        if c ^ (stream // 2):
            pairs.append((i, index(h, z, x + step, l, c)))
        else:
            pairs.append((i, index(h, z + step, x, l, c)))
    return hbm(lax.ppermute(value, AXES, pairs))


def across(value, stream):
    pairs = []
    for i in range(128):
        h, z, x, l, c = coords(i)
        role = c ^ (stream // 2)
        pairs.append((i, index(h ^ 1 ^ role, z, x, l ^ role, c)))
    return hbm(lax.ppermute(value, AXES, pairs))


def after(value, *others):
    return lax.optimization_barrier((value, *others))[0]


VMEM = pl.BlockSpec(memory_space=pltpu.VMEM)
ANYWHERE = pl.BlockSpec(memory_space=pltpu.HBM)


def stacked(pieces):
    n = len(pieces)

    def kernel(*refs):
        for j in range(n):
            refs[n][j] = refs[j][...]

    return pl.pallas_call(
        kernel,
        out_shape=jax.ShapeDtypeStruct((n, *pieces[0].shape), pieces[0].dtype),
        in_specs=[VMEM] * n,
        out_specs=VMEM,
        name="stacked",
    )(*pieces)


def product(pieces, blocks, role, core, rows, columns, total, last):
    n = len(pieces)
    width, half = 512, 256

    def kernel(at, *refs):
        chunks, (r_own, r_other, l_own, l_other), rest = refs[:n], refs[n : n + 4], refs[n + 4 :]
        out, a, b, sems = rest[-4:]
        role, core = at[n], at[n + 1]

        def copies_of(role, j):
            k, chunk = j * width, chunks[j]
            if role == 0:
                mine = pl.ds(pl.multiple_of(core * half, half), half)
                theirs = pl.ds(pl.multiple_of((1 - core) * half, half), half)
                pairs = [
                    (r_own.at[at[j]], a.at[:, k : k + half]),
                    (r_other.at[at[j]], a.at[:, k + half : k + width]),
                    (chunk.at[mine, :], b.at[k : k + half, :]),
                    (chunk.at[theirs, :], b.at[k + half : k + width, :]),
                ]
            else:
                block = pl.ds(pl.multiple_of(at[j] * width, width), width)
                pairs = [
                    (chunk, a.at[:, k : k + width]),
                    (l_own.at[block, :], b.at[k : k + width, :half]),
                    (l_other.at[block, :], b.at[k : k + width, half:]),
                ]
            return [
                pltpu.make_async_copy(src, dst, sems.at[4 * j + i])
                for i, (src, dst) in enumerate(pairs)
            ]

        for r in (0, 1):

            @pl.when(role == r)
            def _():
                for j in range(n):
                    for copy in copies_of(r, j):
                        copy.start()

        for j in range(0, n, 2):
            for r in (0, 1):

                @pl.when(role == r)
                def _():
                    for i in range(j, j + 2):
                        for copy in copies_of(r, i):
                            copy.wait()

            k = slice(j * width, (j + 2) * width)
            value = jnp.dot(a[:, k], b[k, :], preferred_element_type=jnp.float32)
            if j == 0 and total is not None:
                value = value + rest[0][...]
            if j > 0:
                value = value + rest[-5][...]
            if j + 2 < n:
                rest[-5][...] = value
            else:
                out[...] = value.astype(out.dtype)

    def body(at, *refs):
        ins, out, acc, a, b, sems = refs[:-5], *refs[-5:]
        kernel(at, *ins, acc, out, a, b, sems)

    whole = pl.BlockSpec((width, width), lambda i, at: (0, 0))
    totals = [] if total is None else [total]
    return pl.pallas_call(
        body,
        out_shape=jax.ShapeDtypeStruct((width, width), jnp.bfloat16 if last else jnp.float32),
        grid_spec=pltpu.PrefetchScalarGridSpec(
            num_scalar_prefetch=1,
            grid=(1,),
            in_specs=[ANYWHERE] * (n + 4) + [whole] * len(totals),
            out_specs=whole,
            scratch_shapes=[
                pltpu.VMEM((width, width), jnp.float32),
                pltpu.VMEM((width, n * width), jnp.bfloat16),
                pltpu.VMEM((n * width, width), jnp.bfloat16),
                pltpu.SemaphoreType.DMA((4 * n,)),
            ],
        ),
        compiler_params=pltpu.CompilerParams(vmem_limit_bytes=24 << 20),
        name="product",
    )(jnp.stack([*blocks, role, core]).astype(jnp.int32), *map(hbm, (*pieces, *rows, *columns)), *totals)


def per_device(outputs, run_precision, line_precision):
    run, cell = lax.axis_index("run"), lax.axis_index("cell")
    core, x, yl = cell & 1, cell >> 2, cell >> 1 & 1
    first = core == 0

    r_own = hbm(run_precision)
    r_below, r_above = hbm(send(r_own, dx=1)), hbm(send(r_own, dx=-1))
    r_partner = hbm(send(r_own, yl=1))

    lines = jnp.transpose(outputs, (1, 0, 2))
    mine = lax.dynamic_slice_in_dim(lines, 2 * core, 2, 0)
    theirs = send(lax.dynamic_slice_in_dim(lines, 2 - 2 * core, 2, 0), core=1)
    chunk = jnp.concatenate([jnp.where(first, mine, theirs), jnp.where(first, theirs, mine)], axis=2)
    l_own = hbm(line_precision)
    columns = (l_own, hbm(send(l_own, core=1)))

    own = [hbm(chunk[0]), hbm(chunk[1])]
    own = [*lax.optimization_barrier((*own, columns[1]))[:2], None, None]
    lo, hi, far, partner, p_lo, p_hi, p_far = ([None] * 4 for _ in range(7))

    def apply(s, pieces, offsets, total, last):
        role = core ^ (s // 2)
        at = []
        for d, p in offsets:
            k = ((run & 4) ^ 4 * p) | (run + d & 3)
            r_at = (((k >> 1) - x & 3) << 1) | ((k & 1) ^ yl)
            l_at = (x + d & 3) << 1 | yl ^ p
            at.append(jnp.where(role == 0, r_at, l_at))
        return product(pieces, at, role, core, rows, columns, total, last)

    def halves(s):
        below, above = -sign(s), sign(s)
        return (
            ([own[s], lo[s], hi[s], far[s]], [(0, 0), (below, 0), (above, 0), (2, 0)]),
            ([partner[s], p_lo[s], p_hi[s], p_far[s]], [(0, 1), (below, 1), (above, 1), (2, 1)]),
        )

    def whole(s):
        (pieces, offsets), (others, more) = halves(s)
        return apply(s, pieces + others, offsets + more, None, True)

    def first_half(s):
        return apply(s, *halves(s)[0], None, False)

    def second_half(s, total):
        return apply(s, *halves(s)[1], total, True)

    partner[0] = across(own[0], 0)
    lo[0], hi[0] = ring(own[0], 0, 1), ring(own[0], 0, -1)
    next_own = after(own[1], lo[0], hi[0])
    lo[1], hi[1] = ring(next_own, 1, 1), ring(next_own, 1, -1)
    r_far = hbm(send(after(r_below, lo[0], hi[0]), dx=1))
    r_p_above = hbm(send(after(r_partner, lo[0], hi[0]), dx=-1))
    r_p_below = hbm(send(after(r_partner, r_far, r_p_above, partner[0]), dx=1))
    r_p_far = hbm(send(after(r_p_above, r_far, partner[0]), dx=-1))
    r_all = hbm(stacked([r_own, r_partner, r_above, r_p_above, r_far, r_p_far, r_below, r_p_below]))

    for s in (0, 2):
        t = s + 1
        if s:
            partner[s] = across(own[s], s)
            lo[s], hi[s] = ring(own[s], s, 1), ring(own[s], s, -1)
            lo[t], hi[t] = ring(own[t], t, 1), ring(own[t], t, -1)
            gate, late = (lo[s], hi[s]), (partner[s],)
        else:
            gate, late = (lo[t], hi[t]), (partner[s], lo[t])
        p_lo[s] = ring(after(partner[s], *gate), s, 1)
        far[s] = ring(after(hi[s], *gate), s, -1)
        partner[t] = across(after(own[t], *late), t)
        far[t] = ring(after(lo[t], hi[t]), t, 1)
        p_hi[s] = ring(after(partner[s], hi[t], lo[t]), s, -1)
        if not s:
            rows = (r_all, hbm(send(after(r_all, far[0], p_lo[0], partner[1]), core=1)))
        p_far[s] = ring(p_lo[s], s, 1)
        p_hi[t] = ring(after(partner[t], far[s]), t, -1)
        p_far[t] = across(after(far[t], partner[t]), t)
        p_lo[t] = ring(after(partner[t], far[t]), t, 1)
        if not s:
            own[2], own[3] = hbm(whole(0)), hbm(whole(1))
    total = first_half(3)
    out_0, out_1 = whole(2), second_half(3, total)
    got_0, got_1 = send(out_0[:, 256:], core=1), send(out_1[:, 256:], core=1)

    kept = jnp.stack([out_0[:, :256], out_1[:, :256]], axis=1)
    got = jnp.stack([got_0, got_1], axis=1)
    return jnp.concatenate([jnp.where(first, kept, got), jnp.where(first, got, kept)], axis=1)


def solution(mesh):
    placed = (P("run", None, "cell"), P("run", "cell"), P(None, "cell"))
    return jax.shard_map(
        per_device, mesh=mesh, in_specs=placed, out_specs=P("run", None, "cell"), check_vma=False
    )
```

```python
import jax
import jax.numpy as jnp
from jax import lax
from jax.experimental import pallas as pl
from jax.experimental.pallas import tpu as pltpu
from jax.sharding import PartitionSpec as P

AXES = ("run", "cell")


def coords(i):
    run, cell = divmod(i, 16)
    return run // 4, run % 4, cell // 4, (cell // 2) % 2, cell % 2


def index(yh, z, x, yl, core):
    return (yh * 4 + z % 4) * 16 + (x % 4) * 4 + yl * 2 + core


def hbm(value):
    return pltpu.with_memory_space_constraint(value, pltpu.HBM)


def send(value, dx=0, yl=0, core=0):
    pairs = []
    for i in range(128):
        h, z, x, l, c = coords(i)
        pairs.append((i, index(h, z, x + dx, l ^ yl, c ^ core)))
    return lax.ppermute(value, AXES, pairs)


def sign(stream):
    return 1 - 2 * (stream // 2)


def ring(value, stream, step):
    step = step * sign(stream)
    pairs = []
    for i in range(128):
        h, z, x, l, c = coords(i)
        if c ^ (stream // 2):
            pairs.append((i, index(h, z, x + step, l, c)))
        else:
            pairs.append((i, index(h, z + step, x, l, c)))
    return hbm(lax.ppermute(value, AXES, pairs))


def across(value, stream):
    pairs = []
    for i in range(128):
        h, z, x, l, c = coords(i)
        role = c ^ (stream // 2)
        pairs.append((i, index(h ^ 1 ^ role, z, x, l ^ role, c)))
    return hbm(lax.ppermute(value, AXES, pairs))


def after(value, *others):
    return lax.optimization_barrier((value, *others))[0]


VMEM = pl.BlockSpec(memory_space=pltpu.VMEM)
ANYWHERE = pl.BlockSpec(memory_space=pltpu.HBM)


def stacked(pieces):
    n = len(pieces)

    def kernel(*refs):
        for j in range(n):
            refs[n][j] = refs[j][...]

    return pl.pallas_call(
        kernel,
        out_shape=jax.ShapeDtypeStruct((n, *pieces[0].shape), pieces[0].dtype),
        in_specs=[VMEM] * n,
        out_specs=VMEM,
        name="stacked",
    )(*pieces)


def product(pieces, blocks, role, core, rows, columns, total, last):
    n = len(pieces)
    width, half = 512, 256

    def kernel(at, *refs):
        chunks, (r_own, r_other, l_own, l_other), rest = refs[:n], refs[n : n + 4], refs[n + 4 :]
        out, a, b, sems = rest[-4:]
        role, core = at[n], at[n + 1]

        def copies_of(role, j):
            k, chunk = j * width, chunks[j]
            if role == 0:
                mine = pl.ds(pl.multiple_of(core * half, half), half)
                theirs = pl.ds(pl.multiple_of((1 - core) * half, half), half)
                pairs = [
                    (r_own.at[at[j]], a.at[:, k : k + half]),
                    (r_other.at[at[j]], a.at[:, k + half : k + width]),
                    (chunk.at[mine, :], b.at[k : k + half, :]),
                    (chunk.at[theirs, :], b.at[k + half : k + width, :]),
                ]
            else:
                block = pl.ds(pl.multiple_of(at[j] * width, width), width)
                pairs = [
                    (chunk, a.at[:, k : k + width]),
                    (l_own.at[block, :], b.at[k : k + width, :half]),
                    (l_other.at[block, :], b.at[k : k + width, half:]),
                ]
            return [
                pltpu.make_async_copy(src, dst, sems.at[4 * j + i])
                for i, (src, dst) in enumerate(pairs)
            ]

        for r in (0, 1):

            @pl.when(role == r)
            def _():
                for j in range(n):
                    for copy in copies_of(r, j):
                        copy.start()

        for j in range(0, n, 2):
            for r in (0, 1):

                @pl.when(role == r)
                def _():
                    for i in range(j, j + 2):
                        for copy in copies_of(r, i):
                            copy.wait()

            k = slice(j * width, (j + 2) * width)
            value = jnp.dot(a[:, k], b[k, :], preferred_element_type=jnp.float32)
            if j == 0 and total is not None:
                value = value + rest[0][...]
            if j > 0:
                value = value + rest[-5][...]
            if j + 2 < n:
                rest[-5][...] = value
            else:
                out[...] = value.astype(out.dtype)

    def body(at, *refs):
        ins, out, acc, a, b, sems = refs[:-5], *refs[-5:]
        kernel(at, *ins, acc, out, a, b, sems)

    whole = pl.BlockSpec((width, width), lambda i, at: (0, 0))
    totals = [] if total is None else [total]
    return pl.pallas_call(
        body,
        out_shape=jax.ShapeDtypeStruct((width, width), jnp.bfloat16 if last else jnp.float32),
        grid_spec=pltpu.PrefetchScalarGridSpec(
            num_scalar_prefetch=1,
            grid=(1,),
            in_specs=[ANYWHERE] * (n + 4) + [whole] * len(totals),
            out_specs=whole,
            scratch_shapes=[
                pltpu.VMEM((width, width), jnp.float32),
                pltpu.VMEM((width, n * width), jnp.bfloat16),
                pltpu.VMEM((n * width, width), jnp.bfloat16),
                pltpu.SemaphoreType.DMA((4 * n,)),
            ],
        ),
        compiler_params=pltpu.CompilerParams(vmem_limit_bytes=24 << 20),
        name="product",
    )(jnp.stack([*blocks, role, core]).astype(jnp.int32), *map(hbm, (*pieces, *rows, *columns)), *totals)


def per_device(outputs, run_precision, line_precision):
    run, cell = lax.axis_index("run"), lax.axis_index("cell")
    core, x, yl = cell & 1, cell >> 2, cell >> 1 & 1
    first = core == 0

    r_own = hbm(run_precision)
    r_below, r_above = hbm(send(r_own, dx=1)), hbm(send(r_own, dx=-1))
    r_partner = hbm(send(r_own, yl=1))

    l_own = hbm(line_precision)
    columns = (l_own, hbm(send(l_own, core=1)))

    lines = jnp.transpose(outputs, (1, 0, 2))
    mine = lax.dynamic_slice_in_dim(lines, 2 * core, 2, 0)
    theirs = lax.dynamic_slice_in_dim(lines, 2 - 2 * core, 2, 0)
    theirs = send(after(theirs, r_below, r_above, r_partner, columns[1]), core=1)
    chunk = jnp.concatenate([jnp.where(first, mine, theirs), jnp.where(first, theirs, mine)], axis=2)
    own = [hbm(chunk[0]), hbm(chunk[1])]
    own = [*lax.optimization_barrier((*own, r_below))[:2], None, None]
    lo, hi, far, partner, p_lo, p_hi, p_far = ([None] * 4 for _ in range(7))

    def apply(s, pieces, offsets, total, last):
        role = core ^ (s // 2)
        at = []
        for d, p in offsets:
            k = ((run & 4) ^ 4 * p) | (run + d & 3)
            r_at = (((k >> 1) - x & 3) << 1) | ((k & 1) ^ yl)
            l_at = (x + d & 3) << 1 | yl ^ p
            at.append(jnp.where(role == 0, r_at, l_at))
        return product(pieces, at, role, core, rows, columns, total, last)

    def halves(s):
        below, above = -sign(s), sign(s)
        return (
            ([own[s], lo[s], hi[s], far[s]], [(0, 0), (below, 0), (above, 0), (2, 0)]),
            ([partner[s], p_lo[s], p_hi[s], p_far[s]], [(0, 1), (below, 1), (above, 1), (2, 1)]),
        )

    def whole(s):
        (pieces, offsets), (others, more) = halves(s)
        return apply(s, pieces + others, offsets + more, None, True)

    def first_half(s):
        return apply(s, *halves(s)[0], None, False)

    def second_half(s, total):
        return apply(s, *halves(s)[1], total, True)

    r_far, r_p_above = hbm(send(after(r_below, own[0]), dx=1)), hbm(send(after(r_partner, own[0]), dx=-1))
    partner[0] = across(own[0], 0)
    lo[0], hi[0] = ring(own[0], 0, 1), ring(own[0], 0, -1)
    started = (r_far, r_p_above, lo[0], hi[0])
    r_p_below = hbm(send(after(r_partner, *started), dx=1))
    r_p_far = hbm(send(after(r_p_above, *started), dx=-1))
    next_own = after(own[1], *started)
    lo[1], hi[1] = ring(next_own, 1, 1), ring(next_own, 1, -1)
    r_pieces = [r_own, r_partner, r_above, r_p_above, r_far, r_p_far, r_below, r_p_below]
    r_all = hbm(stacked([after(r_own, lo[1], hi[1], partner[0]), *r_pieces[1:]]))
    rows = (r_all, hbm(send(r_all, core=1)))

    for s in (0, 2):
        t = s + 1
        if s:
            partner[s] = across(own[s], s)
            lo[s], hi[s] = ring(own[s], s, 1), ring(own[s], s, -1)
            lo[t], hi[t] = ring(own[t], t, 1), ring(own[t], t, -1)
            gate, late = (lo[s], hi[s]), (partner[s],)
        else:
            gate, late = (hi[s], r_p_below, r_p_far), (partner[s], r_p_below, r_p_far)
        p_lo[s] = ring(after(partner[s], *gate), s, 1)
        far[s] = ring(after(hi[s], *gate), s, -1)
        partner[t] = across(after(own[t], *late), t)
        far[t] = ring(after(lo[t], hi[t]), t, 1)
        p_hi[s] = ring(after(partner[s], hi[t], lo[t]), s, -1)
        p_far[s] = ring(p_lo[s], s, 1)
        p_hi[t] = ring(after(partner[t], far[s]), t, -1)
        p_far[t] = across(after(far[t], partner[t]), t)
        p_lo[t] = ring(after(partner[t], far[t]), t, 1)
        if not s:
            own[2], own[3] = hbm(whole(0)), hbm(whole(1))
    total = first_half(3)
    out_0, out_1 = whole(2), second_half(3, total)
    got_0, got_1 = send(out_0[:, 256:], core=1), send(out_1[:, 256:], core=1)

    kept = jnp.stack([out_0[:, :256], out_1[:, :256]], axis=1)
    got = jnp.stack([got_0, got_1], axis=1)
    return jnp.concatenate([jnp.where(first, kept, got), jnp.where(first, got, kept)], axis=1)


def solution(mesh):
    placed = (P("run", None, "cell"), P("run", "cell"), P(None, "cell"))
    return jax.shard_map(
        per_device, mesh=mesh, in_specs=placed, out_specs=P("run", None, "cell"), check_vma=False
    )
```

```python
import jax
import jax.numpy as jnp
from jax import lax
from jax.experimental import pallas as pl
from jax.experimental.pallas import tpu as pltpu
from jax.sharding import PartitionSpec as P

AXES = ("run", "cell")


def coords(i):
    run, cell = divmod(i, 16)
    return run // 4, run % 4, cell // 4, (cell // 2) % 2, cell % 2


def index(yh, z, x, yl, core):
    return (yh * 4 + z % 4) * 16 + (x % 4) * 4 + yl * 2 + core


def hbm(value):
    return pltpu.with_memory_space_constraint(value, pltpu.HBM)


def send(value, dx=0, yl=0, core=0):
    pairs = []
    for i in range(128):
        h, z, x, l, c = coords(i)
        pairs.append((i, index(h, z, x + dx, l ^ yl, c ^ core)))
    return lax.ppermute(value, AXES, pairs)


def sign(stream):
    return 1 - 2 * (stream // 2)


def ring(value, stream, step):
    step = step * sign(stream)
    pairs = []
    for i in range(128):
        h, z, x, l, c = coords(i)
        if c ^ (stream // 2):
            pairs.append((i, index(h, z, x + step, l, c)))
        else:
            pairs.append((i, index(h, z + step, x, l, c)))
    return hbm(lax.ppermute(value, AXES, pairs))


def across(value, stream):
    pairs = []
    for i in range(128):
        h, z, x, l, c = coords(i)
        role = c ^ (stream // 2)
        pairs.append((i, index(h ^ 1 ^ role, z, x, l ^ role, c)))
    return hbm(lax.ppermute(value, AXES, pairs))


def after(value, *others):
    return lax.optimization_barrier((value, *others))[0]


VMEM = pl.BlockSpec(memory_space=pltpu.VMEM)
ANYWHERE = pl.BlockSpec(memory_space=pltpu.HBM)
FREE = pl.BlockSpec(memory_space=pl.ANY)


def stacked(pieces):
    n = len(pieces)

    def kernel(*refs):
        copies = [
            pltpu.make_async_copy(refs[j], refs[n].at[j], refs[n + 1].at[j]) for j in range(n)
        ]
        for copy in copies:
            copy.start()
        for copy in copies:
            copy.wait()

    return pl.pallas_call(
        kernel,
        out_shape=jax.ShapeDtypeStruct((n, *pieces[0].shape), pieces[0].dtype),
        in_specs=[pl.BlockSpec(memory_space=pl.ANY)] * n,
        out_specs=VMEM,
        scratch_shapes=[pltpu.SemaphoreType.DMA((n,))],
        name="stacked",
    )(*pieces)


def product(pieces, blocks, role, core, rows, columns, total, last):
    n = len(pieces)
    width, half = 512, 256

    def kernel(at, *refs):
        chunks, (r_own, r_other, l_own, l_other), rest = refs[:n], refs[n : n + 4], refs[n + 4 :]
        out, a, b, sems = rest[-4:]
        role, core = at[n], at[n + 1]

        def copies_of(role, j):
            k, chunk = j * width, chunks[j]
            if role == 0:
                mine = pl.ds(pl.multiple_of(core * half, half), half)
                theirs = pl.ds(pl.multiple_of((1 - core) * half, half), half)
                pairs = [
                    (r_own.at[at[j]], a.at[:, k : k + half]),
                    (r_other.at[at[j]], a.at[:, k + half : k + width]),
                    (chunk.at[mine, :], b.at[k : k + half, :]),
                    (chunk.at[theirs, :], b.at[k + half : k + width, :]),
                ]
            else:
                block = pl.ds(pl.multiple_of(at[j] * width, width), width)
                pairs = [
                    (chunk, a.at[:, k : k + width]),
                    (l_own.at[block, :], b.at[k : k + width, :half]),
                    (l_other.at[block, :], b.at[k : k + width, half:]),
                ]
            return [
                pltpu.make_async_copy(src, dst, sems.at[4 * j + i])
                for i, (src, dst) in enumerate(pairs)
            ]

        for r in (0, 1):

            @pl.when(role == r)
            def _():
                for j in range(n):
                    for copy in copies_of(r, j):
                        copy.start()

        for j in range(0, n, 2):
            top = min(j + 2, n)
            for r in (0, 1):

                @pl.when(role == r)
                def _():
                    for i in range(j, top):
                        for copy in copies_of(r, i):
                            copy.wait()

            k = slice(j * width, top * width)
            value = jnp.dot(a[:, k], b[k, :], preferred_element_type=jnp.float32)
            if j == 0 and total is not None:
                value = value + rest[0][...]
            if j > 0:
                value = value + rest[-5][...]
            if top < n:
                rest[-5][...] = value
            else:
                out[...] = value.astype(out.dtype)

    def body(at, *refs):
        ins, out, acc, a, b, sems = refs[:-5], *refs[-5:]
        kernel(at, *ins, acc, out, a, b, sems)

    whole = pl.BlockSpec((width, width), lambda i, at: (0, 0))
    totals = [] if total is None else [total]
    return pl.pallas_call(
        body,
        out_shape=jax.ShapeDtypeStruct((width, width), jnp.bfloat16 if last else jnp.float32),
        grid_spec=pltpu.PrefetchScalarGridSpec(
            num_scalar_prefetch=1,
            grid=(1,),
            in_specs=[ANYWHERE] * (n + 1) + [FREE] + [ANYWHERE] * 2 + [whole] * len(totals),
            out_specs=whole,
            scratch_shapes=[
                pltpu.VMEM((width, width), jnp.float32),
                pltpu.VMEM((width, n * width), jnp.bfloat16),
                pltpu.VMEM((n * width, width), jnp.bfloat16),
                pltpu.SemaphoreType.DMA((4 * n,)),
            ],
        ),
        compiler_params=pltpu.CompilerParams(vmem_limit_bytes=24 << 20),
        name="product",
    )(jnp.stack([*blocks, role, core]).astype(jnp.int32), *map(hbm, pieces), hbm(rows[0]), rows[1], *map(hbm, columns), *totals)


def per_device(outputs, run_precision, line_precision):
    run, cell = lax.axis_index("run"), lax.axis_index("cell")
    core, x, yl = cell & 1, cell >> 2, cell >> 1 & 1
    first = core == 0

    r_own = run_precision
    r_below, r_above = send(r_own, dx=1), send(r_own, dx=-1)
    r_partner = send(r_own, yl=1)

    l_own = hbm(line_precision)
    columns = (l_own, hbm(send(l_own, core=1)))

    lines = jnp.transpose(outputs, (1, 0, 2))
    mine = lax.dynamic_slice_in_dim(lines, 2 * core, 2, 0)
    theirs = lax.dynamic_slice_in_dim(lines, 2 - 2 * core, 2, 0)
    theirs = send(after(theirs, r_below, r_above, r_partner, columns[1]), core=1)
    chunk = jnp.concatenate([jnp.where(first, mine, theirs), jnp.where(first, theirs, mine)], axis=2)
    own = [hbm(chunk[0]), hbm(chunk[1])]
    own = [*lax.optimization_barrier((*own, r_below))[:2], None, None]
    lo, hi, far, partner, p_lo, p_hi, p_far = ([None] * 4 for _ in range(7))

    def apply(s, pieces, offsets, total, last):
        role = core ^ (s // 2)
        at = []
        for d, p in offsets:
            k = ((run & 4) ^ 4 * p) | (run + d & 3)
            r_at = (((k >> 1) - x & 3) << 1) | ((k & 1) ^ yl)
            l_at = (x + d & 3) << 1 | yl ^ p
            at.append(jnp.where(role == 0, r_at, l_at))
        return product(pieces, at, role, core, rows, columns, total, last)

    def halves(s):
        below, above = -sign(s), sign(s)
        return (
            ([own[s], lo[s], hi[s], far[s]], [(0, 0), (below, 0), (above, 0), (2, 0)]),
            ([partner[s], p_lo[s], p_hi[s], p_far[s]], [(0, 1), (below, 1), (above, 1), (2, 1)]),
        )

    def whole(s):
        (pieces, offsets), (others, more) = halves(s)
        return apply(s, pieces + others, offsets + more, None, True)

    def first_part(s):
        (pieces, offsets), (others, more) = halves(s)
        return apply(s, pieces + others[:1], offsets + more[:1], None, False)

    def last_part(s, total):
        others, more = halves(s)[1]
        return apply(s, others[1:], more[1:], total, True)

    r_far, r_p_above = send(after(r_below, own[0]), dx=1), send(after(r_partner, own[0]), dx=-1)
    partner[0] = across(own[0], 0)
    lo[0], hi[0] = ring(own[0], 0, 1), ring(own[0], 0, -1)
    started = (r_far, r_p_above, lo[0], hi[0])
    r_p_below = send(after(r_partner, *started), dx=1)
    r_p_far = send(after(r_p_above, *started), dx=-1)
    next_own = after(own[1], lo[0], hi[0])
    lo[1], hi[1] = ring(next_own, 1, 1), ring(next_own, 1, -1)
    r_pieces = [r_own, r_partner, r_above, r_p_above, r_far, r_p_far, r_below, r_p_below]
    r_all = hbm(stacked([after(r_own, lo[1], hi[1], partner[0]), *r_pieces[1:]]))
    rows = (r_all, send(r_all, core=1))

    for s in (0, 2):
        t = s + 1
        if s:
            partner[s] = across(own[s], s)
            lo[s], hi[s] = ring(own[s], s, 1), ring(own[s], s, -1)
            lo[t], hi[t] = ring(own[t], t, 1), ring(own[t], t, -1)
            gate, late = (lo[s], hi[s]), (partner[s],)
        else:
            gate, late = (hi[s], r_p_below, r_p_far), (partner[s], r_p_below, r_p_far)
        p_lo[s] = ring(after(partner[s], *gate), s, 1)
        far[s] = ring(after(hi[s], *gate), s, -1)
        partner[t] = across(after(own[t], *late), t)
        far[t] = ring(after(lo[t], hi[t]), t, 1)
        p_hi[s] = ring(after(partner[s], hi[t], lo[t]), s, -1)
        p_far[s] = ring(p_lo[s], s, 1)
        p_hi[t] = ring(after(partner[t], far[s]), t, -1)
        p_far[t] = across(far[t] if s else after(far[t], partner[t]), t)
        p_lo[t] = ring(after(partner[t], far[t]), t, 1)
        if not s:
            own[2], own[3] = hbm(whole(0)), hbm(whole(1))
    total = first_part(3)
    out_0, out_1 = whole(2), last_part(3, total)
    got_0, got_1 = send(out_0[:, 256:], core=1), send(out_1[:, 256:], core=1)

    kept = jnp.stack([out_0[:, :256], out_1[:, :256]], axis=1)
    got = jnp.stack([got_0, got_1], axis=1)
    return jnp.concatenate([jnp.where(first, kept, got), jnp.where(first, got, kept)], axis=1)


def solution(mesh):
    placed = (P("run", None, "cell"), P("run", "cell"), P(None, "cell"))
    return jax.shard_map(
        per_device, mesh=mesh, in_specs=placed, out_specs=P("run", None, "cell"), check_vma=False
    )
```

```python
import jax
import jax.numpy as jnp
from jax import lax
from jax.experimental import pallas as pl
from jax.experimental.pallas import tpu as pltpu
from jax.sharding import PartitionSpec as P

AXES = ("run", "cell")


def coords(i):
    run, cell = divmod(i, 16)
    return run // 4, run % 4, cell // 4, (cell // 2) % 2, cell % 2


def index(yh, z, x, yl, core):
    return (yh * 4 + z % 4) * 16 + (x % 4) * 4 + yl * 2 + core


def hbm(value):
    return pltpu.with_memory_space_constraint(value, pltpu.HBM)


def send(value, dx=0, yl=0, core=0):
    pairs = []
    for i in range(128):
        h, z, x, l, c = coords(i)
        pairs.append((i, index(h, z, x + dx, l ^ yl, c ^ core)))
    return lax.ppermute(value, AXES, pairs)


def sign(stream):
    return 1 - 2 * (stream // 2)


def ring(value, stream, step):
    step = step * sign(stream)
    pairs = []
    for i in range(128):
        h, z, x, l, c = coords(i)
        if c ^ (stream // 2):
            pairs.append((i, index(h, z, x + step, l, c)))
        else:
            pairs.append((i, index(h, z + step, x, l, c)))
    return hbm(lax.ppermute(value, AXES, pairs))


def across(value, stream):
    pairs = []
    for i in range(128):
        h, z, x, l, c = coords(i)
        role = c ^ (stream // 2)
        pairs.append((i, index(h ^ 1 ^ role, z, x, l ^ role, c)))
    return hbm(lax.ppermute(value, AXES, pairs))


def after(value, *others):
    return lax.optimization_barrier((value, *others))[0]


VMEM = pl.BlockSpec(memory_space=pltpu.VMEM)
ANYWHERE = pl.BlockSpec(memory_space=pltpu.HBM)
FREE = pl.BlockSpec(memory_space=pl.ANY)


def stacked(pieces):
    n = len(pieces)

    def kernel(*refs):
        out, held, arrive, leave = refs[n:]
        ins = [pltpu.make_async_copy(refs[j], held.at[j], arrive.at[j]) for j in range(n)]
        outs = [pltpu.make_async_copy(held.at[j], out.at[j], leave.at[j]) for j in range(n)]
        for copy in ins:
            copy.start()
        for j in range(n):
            ins[j].wait()
            outs[j].start()
        for copy in outs:
            copy.wait()

    return pl.pallas_call(
        kernel,
        out_shape=jax.ShapeDtypeStruct((n, *pieces[0].shape), pieces[0].dtype),
        in_specs=[pl.BlockSpec(memory_space=pl.ANY)] * n,
        out_specs=ANYWHERE,
        scratch_shapes=[
            pltpu.VMEM((n, *pieces[0].shape), pieces[0].dtype),
            pltpu.SemaphoreType.DMA((n,)),
            pltpu.SemaphoreType.DMA((n,)),
        ],
        name="stacked",
    )(*pieces)


def product(pieces, blocks, role, core, rows, columns, total, last):
    n = len(pieces)
    width, half = 512, 256

    def kernel(at, *refs):
        chunks, (r_own, r_other, l_own, l_other), rest = refs[:n], refs[n : n + 4], refs[n + 4 :]
        out, a, b, sems = rest[-4:]
        role, core = at[n], at[n + 1]

        def copies_of(role, j):
            k, chunk = j * width, chunks[j]
            if role == 0:
                mine = pl.ds(pl.multiple_of(core * half, half), half)
                theirs = pl.ds(pl.multiple_of((1 - core) * half, half), half)
                pairs = [
                    (r_own.at[at[j]], a.at[:, k : k + half]),
                    (r_other.at[at[j]], a.at[:, k + half : k + width]),
                    (chunk.at[mine, :], b.at[k : k + half, :]),
                    (chunk.at[theirs, :], b.at[k + half : k + width, :]),
                ]
            else:
                block = pl.ds(pl.multiple_of(at[j] * width, width), width)
                pairs = [
                    (chunk, a.at[:, k : k + width]),
                    (l_own.at[block, :], b.at[k : k + width, :half]),
                    (l_other.at[block, :], b.at[k : k + width, half:]),
                ]
            return [
                pltpu.make_async_copy(src, dst, sems.at[4 * j + i])
                for i, (src, dst) in enumerate(pairs)
            ]

        for r in (0, 1):

            @pl.when(role == r)
            def _():
                for j in range(n):
                    for copy in copies_of(r, j):
                        copy.start()

        for j in range(0, n, 2):
            top = min(j + 2, n)
            for r in (0, 1):

                @pl.when(role == r)
                def _():
                    for i in range(j, top):
                        for copy in copies_of(r, i):
                            copy.wait()

            k = slice(j * width, top * width)
            value = jnp.dot(a[:, k], b[k, :], preferred_element_type=jnp.float32)
            if j == 0 and total is not None:
                value = value + rest[0][...]
            if j > 0:
                value = value + rest[-5][...]
            if top < n:
                rest[-5][...] = value
            else:
                out[...] = value.astype(out.dtype)

    def body(at, *refs):
        ins, out, acc, a, b, sems = refs[:-5], *refs[-5:]
        kernel(at, *ins, acc, out, a, b, sems)

    whole = pl.BlockSpec((width, width), lambda i, at: (0, 0))
    totals = [] if total is None else [total]
    return pl.pallas_call(
        body,
        out_shape=jax.ShapeDtypeStruct((width, width), jnp.bfloat16 if last else jnp.float32),
        grid_spec=pltpu.PrefetchScalarGridSpec(
            num_scalar_prefetch=1,
            grid=(1,),
            in_specs=[ANYWHERE] * (n + 1) + [FREE] + [ANYWHERE] * 2 + [whole] * len(totals),
            out_specs=whole,
            scratch_shapes=[
                pltpu.VMEM((width, width), jnp.float32),
                pltpu.VMEM((width, n * width), jnp.bfloat16),
                pltpu.VMEM((n * width, width), jnp.bfloat16),
                pltpu.SemaphoreType.DMA((4 * n,)),
            ],
        ),
        compiler_params=pltpu.CompilerParams(vmem_limit_bytes=24 << 20),
        name="product",
    )(jnp.stack([*blocks, role, core]).astype(jnp.int32), *map(hbm, pieces), hbm(rows[0]), rows[1], *map(hbm, columns), *totals)


def per_device(outputs, run_precision, line_precision):
    run, cell = lax.axis_index("run"), lax.axis_index("cell")
    core, x, yl = cell & 1, cell >> 2, cell >> 1 & 1
    first = core == 0

    r_own = run_precision
    r_below, r_above = send(r_own, dx=1), send(r_own, dx=-1)
    r_partner = send(r_own, yl=1)

    l_own = hbm(line_precision)
    columns = (l_own, hbm(send(l_own, core=1)))

    lines = jnp.transpose(outputs, (1, 0, 2))
    mine = lax.dynamic_slice_in_dim(lines, 2 * core, 2, 0)
    theirs = lax.dynamic_slice_in_dim(lines, 2 - 2 * core, 2, 0)
    theirs = send(after(theirs, r_below, r_above, r_partner, columns[1]), core=1)
    chunk = jnp.concatenate([jnp.where(first, mine, theirs), jnp.where(first, theirs, mine)], axis=2)
    own = [hbm(chunk[0]), hbm(chunk[1])]
    own = [*lax.optimization_barrier((*own, r_below))[:2], None, None]
    lo, hi, far, partner, p_lo, p_hi, p_far = ([None] * 4 for _ in range(7))

    def apply(s, pieces, offsets, total, last):
        role = core ^ (s // 2)
        at = []
        for d, p in offsets:
            k = ((run & 4) ^ 4 * p) | (run + d & 3)
            r_at = (((k >> 1) - x & 3) << 1) | ((k & 1) ^ yl)
            l_at = (x + d & 3) << 1 | yl ^ p
            at.append(jnp.where(role == 0, r_at, l_at))
        return product(pieces, at, role, core, rows, columns, total, last)

    def halves(s):
        below, above = -sign(s), sign(s)
        return (
            ([own[s], lo[s], hi[s], far[s]], [(0, 0), (below, 0), (above, 0), (2, 0)]),
            ([partner[s], p_lo[s], p_hi[s], p_far[s]], [(0, 1), (below, 1), (above, 1), (2, 1)]),
        )

    def whole(s):
        (pieces, offsets), (others, more) = halves(s)
        return apply(s, pieces + others, offsets + more, None, True)

    def first_part(s):
        (pieces, offsets), (others, more) = halves(s)
        return apply(s, pieces + others[:1], offsets + more[:1], None, False)

    def last_part(s, total):
        others, more = halves(s)[1]
        return apply(s, others[1:], more[1:], total, True)

    r_far, r_p_above = send(after(r_below, own[0]), dx=1), send(after(r_partner, own[0]), dx=-1)
    partner[0] = across(own[0], 0)
    lo[0], hi[0] = ring(own[0], 0, 1), ring(own[0], 0, -1)
    started = (r_far, r_p_above, lo[0], hi[0])
    r_p_below = send(after(r_partner, lo[0], hi[0]), dx=1)
    r_p_far = send(after(r_p_above, *started), dx=-1)
    next_own = after(own[1], lo[0], hi[0])
    lo[1], hi[1] = ring(next_own, 1, 1), ring(next_own, 1, -1)
    r_pieces = [r_own, r_partner, r_above, r_p_above, r_far, r_p_far, r_below, r_p_below]
    r_all = hbm(stacked([after(r_own, lo[1], hi[1], partner[0]), *r_pieces[1:]]))
    rows = (r_all, send(r_all, core=1))

    for s in (0, 2):
        t = s + 1
        if s:
            partner[s] = across(own[s], s)
            lo[s], hi[s] = ring(own[s], s, 1), ring(own[s], s, -1)
            lo[t], hi[t] = ring(own[t], t, 1), ring(own[t], t, -1)
            gate, late = (lo[s], hi[s]), ()
        else:
            gate, late = (hi[s], r_p_below, r_p_far), (partner[s], r_p_below, r_p_far)
        p_lo[s] = ring(after(partner[s], *gate), s, 1)
        far[s] = ring(after(hi[s], *gate), s, -1)
        partner[t] = across(after(own[t], *late), t)
        far[t] = ring(after(lo[t], hi[t]), t, 1)
        p_hi[s] = ring(after(partner[s], hi[t], lo[t]), s, -1)
        p_far[s] = ring(p_lo[s], s, 1)
        p_hi[t] = ring(after(partner[t], far[s]), t, -1)
        p_far[t] = across(far[t] if s else after(far[t], partner[t]), t)
        p_lo[t] = ring(after(partner[t], far[t]), t, 1)
        if not s:
            own[2], own[3] = hbm(whole(0)), hbm(whole(1))
    total = first_part(3)
    out_0, out_1 = whole(2), last_part(3, total)
    got_0, got_1 = send(out_0[:, 256:], core=1), send(out_1[:, 256:], core=1)

    kept = jnp.stack([out_0[:, :256], out_1[:, :256]], axis=1)
    got = jnp.stack([got_0, got_1], axis=1)
    return jnp.concatenate([jnp.where(first, kept, got), jnp.where(first, got, kept)], axis=1)


def solution(mesh):
    placed = (P("run", None, "cell"), P("run", "cell"), P(None, "cell"))
    return jax.shard_map(
        per_device, mesh=mesh, in_specs=placed, out_specs=P("run", None, "cell"), check_vma=False
    )
```

```python
import jax
import jax.numpy as jnp
from jax import lax
from jax.experimental import pallas as pl
from jax.experimental.pallas import tpu as pltpu
from jax.sharding import PartitionSpec as P

AXES = ("run", "cell")


def coords(i):
    run, cell = divmod(i, 16)
    return run // 4, run % 4, cell // 4, (cell // 2) % 2, cell % 2


def index(yh, z, x, yl, core):
    return (yh * 4 + z % 4) * 16 + (x % 4) * 4 + yl * 2 + core


def hbm(value):
    return pltpu.with_memory_space_constraint(value, pltpu.HBM)


def send(value, dx=0, yl=0, core=0):
    pairs = []
    for i in range(128):
        h, z, x, l, c = coords(i)
        pairs.append((i, index(h, z, x + dx, l ^ yl, c ^ core)))
    return lax.ppermute(value, AXES, pairs)


def sign(stream):
    return 1 - 2 * (stream // 2)


def ring(value, stream, step):
    step = step * sign(stream)
    pairs = []
    for i in range(128):
        h, z, x, l, c = coords(i)
        if c ^ (stream // 2):
            pairs.append((i, index(h, z, x + step, l, c)))
        else:
            pairs.append((i, index(h, z + step, x, l, c)))
    return hbm(lax.ppermute(value, AXES, pairs))


def across(value, stream):
    pairs = []
    for i in range(128):
        h, z, x, l, c = coords(i)
        role = c ^ (stream // 2)
        pairs.append((i, index(h ^ 1 ^ role, z, x, l ^ role, c)))
    return hbm(lax.ppermute(value, AXES, pairs))


def after(value, *others):
    return lax.optimization_barrier((value, *others))[0]


VMEM = pl.BlockSpec(memory_space=pltpu.VMEM)
ANYWHERE = pl.BlockSpec(memory_space=pltpu.HBM)
FREE = pl.BlockSpec(memory_space=pl.ANY)


def stacked(pieces):
    n = len(pieces)

    def kernel(*refs):
        out, held, arrive, leave = refs[n:]
        ins = [pltpu.make_async_copy(refs[j], held.at[j], arrive.at[j]) for j in range(n)]
        outs = [pltpu.make_async_copy(held.at[j], out.at[j], leave.at[j]) for j in range(n)]
        for copy in ins:
            copy.start()
        for j in range(n):
            ins[j].wait()
            outs[j].start()
        for copy in outs:
            copy.wait()

    return pl.pallas_call(
        kernel,
        out_shape=jax.ShapeDtypeStruct((n, *pieces[0].shape), pieces[0].dtype),
        in_specs=[pl.BlockSpec(memory_space=pl.ANY)] * n,
        out_specs=ANYWHERE,
        scratch_shapes=[
            pltpu.VMEM((n, *pieces[0].shape), pieces[0].dtype),
            pltpu.SemaphoreType.DMA((n,)),
            pltpu.SemaphoreType.DMA((n,)),
        ],
        name="stacked",
    )(*pieces)


def product(pieces, blocks, role, core, rows, columns, total, last):
    n = len(pieces)
    width, half = 512, 256

    def kernel(at, *refs):
        chunks, (r_own, r_other, l_own, l_other), rest = refs[:n], refs[n : n + 4], refs[n + 4 :]
        out, a, b, sems = rest[-4:]
        role, core = at[n], at[n + 1]

        def copies_of(role, j):
            k, chunk = j * width, chunks[j]
            if role == 0:
                mine = pl.ds(pl.multiple_of(core * half, half), half)
                theirs = pl.ds(pl.multiple_of((1 - core) * half, half), half)
                pairs = [
                    (r_own.at[at[j]], a.at[:, k : k + half]),
                    (r_other.at[at[j]], a.at[:, k + half : k + width]),
                    (chunk.at[mine, :], b.at[k : k + half, :]),
                    (chunk.at[theirs, :], b.at[k + half : k + width, :]),
                ]
            else:
                block = pl.ds(pl.multiple_of(at[j] * width, width), width)
                pairs = [
                    (chunk, a.at[:, k : k + width]),
                    (l_own.at[block, :], b.at[k : k + width, :half]),
                    (l_other.at[block, :], b.at[k : k + width, half:]),
                ]
            return [
                pltpu.make_async_copy(src, dst, sems.at[4 * j + i])
                for i, (src, dst) in enumerate(pairs)
            ]

        for r in (0, 1):

            @pl.when(role == r)
            def _():
                for j in range(n):
                    for copy in copies_of(r, j):
                        copy.start()

        for j in range(0, n, 2):
            top = min(j + 2, n)
            for r in (0, 1):

                @pl.when(role == r)
                def _():
                    for i in range(j, top):
                        for copy in copies_of(r, i):
                            copy.wait()

            k = slice(j * width, top * width)
            value = jnp.dot(a[:, k], b[k, :], preferred_element_type=jnp.float32)
            if j == 0 and total is not None:
                value = value + rest[0][...]
            if j > 0:
                value = value + rest[-5][...]
            if top < n:
                rest[-5][...] = value
            else:
                out[...] = value.astype(out.dtype)

    def body(at, *refs):
        ins, out, acc, a, b, sems = refs[:-5], *refs[-5:]
        kernel(at, *ins, acc, out, a, b, sems)

    whole = pl.BlockSpec((width, width), lambda i, at: (0, 0))
    totals = [] if total is None else [total]
    return pl.pallas_call(
        body,
        out_shape=jax.ShapeDtypeStruct((width, width), jnp.bfloat16 if last else jnp.float32),
        grid_spec=pltpu.PrefetchScalarGridSpec(
            num_scalar_prefetch=1,
            grid=(1,),
            in_specs=[ANYWHERE] * (n + 1) + [FREE] + [ANYWHERE] * 2 + [whole] * len(totals),
            out_specs=whole,
            scratch_shapes=[
                pltpu.VMEM((width, width), jnp.float32),
                pltpu.VMEM((width, n * width), jnp.bfloat16),
                pltpu.VMEM((n * width, width), jnp.bfloat16),
                pltpu.SemaphoreType.DMA((4 * n,)),
            ],
        ),
        compiler_params=pltpu.CompilerParams(vmem_limit_bytes=24 << 20),
        name="product",
    )(jnp.stack([*blocks, role, core]).astype(jnp.int32), *map(hbm, pieces), hbm(rows[0]), rows[1], *map(hbm, columns), *totals)


def per_device(outputs, run_precision, line_precision):
    run, cell = lax.axis_index("run"), lax.axis_index("cell")
    core, x, yl = cell & 1, cell >> 2, cell >> 1 & 1
    first = core == 0

    r_own = run_precision
    r_below, r_above = send(r_own, dx=1), send(r_own, dx=-1)
    r_partner = send(r_own, yl=1)

    l_own = hbm(line_precision)
    columns = (l_own, hbm(send(l_own, core=1)))

    lines = jnp.transpose(outputs, (1, 0, 2))
    mine = lax.dynamic_slice_in_dim(lines, 2 * core, 2, 0)
    theirs = lax.dynamic_slice_in_dim(lines, 2 - 2 * core, 2, 0)
    theirs = send(after(theirs, r_below, r_above, r_partner, columns[1]), core=1)
    chunk = jnp.concatenate([jnp.where(first, mine, theirs), jnp.where(first, theirs, mine)], axis=2)
    own = [hbm(chunk[0]), hbm(chunk[1])]
    own = [*lax.optimization_barrier((*own, r_below))[:2], None, None]
    lo, hi, far, partner, p_lo, p_hi, p_far = ([None] * 4 for _ in range(7))

    def apply(s, pieces, offsets, total, last):
        role = core ^ (s // 2)
        at = []
        for d, p in offsets:
            k = ((run & 4) ^ 4 * p) | (run + d & 3)
            r_at = (((k >> 1) - x & 3) << 1) | ((k & 1) ^ yl)
            l_at = (x + d & 3) << 1 | yl ^ p
            at.append(jnp.where(role == 0, r_at, l_at))
        return product(pieces, at, role, core, rows, columns, total, last)

    def halves(s):
        below, above = -sign(s), sign(s)
        return (
            ([own[s], lo[s], hi[s], far[s]], [(0, 0), (below, 0), (above, 0), (2, 0)]),
            ([partner[s], p_lo[s], p_hi[s], p_far[s]], [(0, 1), (below, 1), (above, 1), (2, 1)]),
        )

    def whole(s):
        (pieces, offsets), (others, more) = halves(s)
        return apply(s, pieces + others, offsets + more, None, True)

    def first_part(s):
        (pieces, offsets), (others, more) = halves(s)
        return apply(s, pieces + [others[0], others[2]], offsets + [more[0], more[2]], None, False)

    def last_part(s, total):
        others, more = halves(s)[1]
        return apply(s, [others[1], others[3]], [more[1], more[3]], total, True)

    r_far, r_p_above = send(after(r_below, own[0]), dx=1), send(after(r_partner, own[0]), dx=-1)
    partner[0] = across(own[0], 0)
    lo[0], hi[0] = ring(own[0], 0, 1), ring(own[0], 0, -1)
    started = (r_far, r_p_above, lo[0], hi[0])
    r_p_below = send(after(r_partner, lo[0], hi[0]), dx=1)
    r_p_far = send(after(r_p_above, *started), dx=-1)
    next_own = after(own[1], lo[0], hi[0])
    lo[1], hi[1] = ring(next_own, 1, 1), ring(next_own, 1, -1)
    r_pieces = [r_own, r_partner, r_above, r_p_above, r_far, r_p_far, r_below, r_p_below]
    r_all = hbm(stacked([after(r_own, lo[1], hi[1], partner[0]), *r_pieces[1:]]))
    rows = (r_all, send(r_all, core=1))

    for s in (0, 2):
        t = s + 1
        if s:
            partner[s] = across(own[s], s)
            lo[s], hi[s] = ring(own[s], s, 1), ring(own[s], s, -1)
            lo[t], hi[t] = ring(own[t], t, 1), ring(own[t], t, -1)
            gate, late = (lo[s], hi[s]), ()
        else:
            gate, late = (hi[s], r_p_below, r_p_far), (partner[s], r_p_below, r_p_far)
        p_lo[s] = ring(after(partner[s], *gate), s, 1)
        far[s] = ring(after(hi[s], *gate), s, -1)
        partner[t] = across(after(own[t], *late), t)
        far[t] = ring(after(lo[t], hi[t]), t, 1)
        p_hi[s] = ring(after(partner[s], hi[t], lo[t]), s, -1)
        p_far[s] = ring(p_lo[s], s, 1)
        p_hi[t] = ring(after(partner[t], far[s]), t, -1)
        p_far[t] = across(far[t] if s else after(far[t], partner[t]), t)
        p_lo[t] = ring(after(partner[t], far[t]), t, 1)
        if not s:
            own[2], own[3] = hbm(whole(0)), hbm(whole(1))
    total = first_part(3)
    out_0, out_1 = whole(2), last_part(3, total)
    got_0, got_1 = send(out_0[:, 256:], core=1), send(out_1[:, 256:], core=1)

    kept = jnp.stack([out_0[:, :256], out_1[:, :256]], axis=1)
    got = jnp.stack([got_0, got_1], axis=1)
    return jnp.concatenate([jnp.where(first, kept, got), jnp.where(first, got, kept)], axis=1)


def solution(mesh):
    placed = (P("run", None, "cell"), P("run", "cell"), P(None, "cell"))
    return jax.shard_map(
        per_device, mesh=mesh, in_specs=placed, out_specs=P("run", None, "cell"), check_vma=False
    )
```
